256 devices in a mesh: tm: 16 (over x_lo, y, core), space: 16 (over x_hi, z).
Axes of the slice: x: 4 (x_hi: 2, x_lo: 2; x = x_hi * 2 + x_lo), y: 4, z: 8, core: 2. Of those that a mesh axis runs over, the one named last changes fastest.
Arguments:
- forward_sketch: float32 [16, 8, 192, 32, 128], P('tm', None, 'space'), may hold values from -8 to 8
- adjoint_sketch: float32 [16, 8, 192, 32, 128], P('tm', None, 'space'), may hold values from -8 to 8
- coefficients: float32 [16, 4, 192, 32, 128], P('tm', None, 'space'), may hold values from -0.15 to 0.15
Outputs:
- forward_basis: float32 [16, 8, 192, 32, 128], P('tm', None, 'space')
- adjoint_basis: float32 [16, 8, 192, 32, 128], P('tm', None, 'space')
- forward_factor: float32 [16, 8, 8], P('tm')
- adjoint_factor: float32 [16, 8, 8], P('tm')
The draws below stay inside these ranges and needn't reach their ends.
All inputs are finite; a program needn't handle non-finite values.
Results may differ from the reference program's by a relative error of at most 0.00011.
Values sent between devices are 32-bit elements; how exact they have to be, the bound alone decides.
No kernel may reach another device: no remote copies, remote signals or barrier semaphores. Data moves between devices by JAX's collectives and lax.ppermute only.
A program may use at most 64 MiB of HBM per device.

```python
import math
import jax
import jax.numpy as jnp
from jax import lax

K = 8
NY = 32
NZ = 128
STEPS = 3
NTS = 16
NX = 192
NCELLS = 786432


def sketch_values(key, label):
    key = jax.random.fold_in(key, label)
    keys = jax.random.split(key, 2)
    shape = (NTS, K, NX, NY, NZ)
    base = jnp.clip(jax.random.normal(keys[0], shape, jnp.float32), -6.0, 6.0)
    vector_scale = jnp.exp(jax.random.uniform(keys[1], (1, K, 1, 1, 1), jnp.float32, math.log(0.5), math.log(2.0)))
    planes = jnp.arange(NX, dtype=jnp.float32)
    ramp = (1.0 + 2.0 * planes / max(NX - 1, 1)).reshape(1, 1, NX, 1, 1)
    values = 0.5 * vector_scale * ramp * base
    return jnp.clip(values, -8.0, 8.0)


def draw_forward_sketch(key, part):
    return sketch_values(key, 11)


def draw_adjoint_sketch(key, part):
    return sketch_values(key, 23)


def level_of(key, shape, shards, least, high):
    level, own = 1.0, jax.random.fold_in(key, 6)
    for dim, blocks in shards:
        steps = jnp.exp(jax.random.uniform(jax.random.fold_in(own, dim), (blocks,), jnp.float32, least / len(shards), high / len(shards)))
        level = level * jnp.repeat(steps, shape[dim] // blocks).reshape([-1 if axis == dim else 1 for axis in range(len(shape))])
    return level


def setup_inputs(seed: int = 0) -> dict:
    splits = jax.random.split(jax.random.key(seed), 4)
    forward_sketch = draw_forward_sketch(jax.random.fold_in(splits[3], 71), 0)
    adjoint_sketch = draw_adjoint_sketch(jax.random.fold_in(splits[3], 71), 0)
    coefficients = jnp.clip(jax.random.uniform(splits[2], (NTS, 4, NX, NY, NZ), jnp.float32, -0.15, 0.15) * level_of(splits[2], (NTS, 4, NX, NY, NZ), ((0, 16), (2, 16)), -0.4, 0.0), -0.15, 0.15)
    return dict(forward_sketch=forward_sketch, adjoint_sketch=adjoint_sketch, coefficients=coefficients)


diffusion = 0.15

def wall_plus(field):
    inner = field[:, :, 1:, :]
    return jnp.concatenate([inner, jnp.zeros_like(field[:, :, :1, :])], axis=2)

def wall_minus(field):
    inner = field[:, :, :-1, :]
    return jnp.concatenate([jnp.zeros_like(field[:, :, :1, :]), inner], axis=2)

def forward_step(field, coeffs):
    plus_x = jnp.roll(field, -1, axis=1)
    minus_x = jnp.roll(field, 1, axis=1)
    plus_y = wall_plus(field)
    minus_y = wall_minus(field)
    plus_z = jnp.roll(field, -1, axis=3)
    minus_z = jnp.roll(field, 1, axis=3)
    center = 1.0 - 6.0 * diffusion - coeffs[3]
    total = center * field + diffusion * (plus_x + minus_x + plus_y + minus_y + plus_z + minus_z)
    total = total - coeffs[0] * (plus_x - minus_x) - coeffs[1] * (plus_y - minus_y)
    return total - coeffs[2] * (plus_z - minus_z)

def adjoint_step(field, coeffs):
    plus_x = jnp.roll(field, -1, axis=1)
    minus_x = jnp.roll(field, 1, axis=1)
    plus_y = wall_plus(field)
    minus_y = wall_minus(field)
    plus_z = jnp.roll(field, -1, axis=3)
    minus_z = jnp.roll(field, 1, axis=3)
    flux_x = coeffs[0] * field
    flux_y = coeffs[1] * field
    flux_z = coeffs[2] * field
    center = 1.0 - 6.0 * diffusion - coeffs[3]
    total = center * field + diffusion * (plus_x + minus_x + plus_y + minus_y + plus_z + minus_z)
    total = total + (jnp.roll(flux_x, -1, axis=1) - jnp.roll(flux_x, 1, axis=1))
    total = total + (wall_plus(flux_y) - wall_minus(flux_y))
    return total + (jnp.roll(flux_z, -1, axis=3) - jnp.roll(flux_z, 1, axis=3))

def run_forward(pair):
    field, coeffs = pair
    for index in range(STEPS):
        field = forward_step(field, coeffs)
    return field

def run_adjoint(pair):
    field, coeffs = pair
    for index in range(STEPS):
        field = adjoint_step(field, coeffs)
    return field

def orthonormalize(block):
    matrix = block.reshape(block.shape[0], -1)
    gram_matrix = jnp.dot(matrix, matrix.T, precision=lax.Precision.HIGHEST, preferred_element_type=matrix.dtype) / NCELLS
    lower_factor = jnp.linalg.cholesky(gram_matrix)
    identity = jnp.eye(block.shape[0], dtype=matrix.dtype)
    inverse = jax.scipy.linalg.solve_triangular(lower_factor, identity, lower=True)
    basis = jnp.dot(inverse, matrix, precision=lax.Precision.HIGHEST, preferred_element_type=matrix.dtype)
    return (basis.reshape(block.shape), lower_factor)

def reference(forward_sketch, adjoint_sketch, coefficients):
    forward_out = lax.map(run_forward, (forward_sketch, coefficients))
    adjoint_out = lax.map(run_adjoint, (adjoint_sketch, coefficients))
    forward_in = jnp.roll(forward_out, 1, axis=0)
    adjoint_in = jnp.roll(adjoint_out, -1, axis=0)
    forward_basis, forward_factor = lax.map(orthonormalize, forward_in)
    adjoint_basis, adjoint_factor = lax.map(orthonormalize, adjoint_in)
    return (forward_basis, adjoint_basis, forward_factor, adjoint_factor)
```

```python
import jax
import jax.numpy as jnp
from jax import lax
from jax.experimental import pallas as pl
from jax.experimental.pallas import tpu as pltpu
from jax.sharding import PartitionSpec as P

diffusion = 0.15
K, NXL, NY, NZ = 8, 12, 32, 128
PAIRS = [(i, j) for i in range(K) for j in range(i + 1)]
NP = len(PAIRS)
F32 = jnp.float32
ANY = pl.BlockSpec(memory_space=pl.ANY)
PAYLOAD = 2 * K * 3 + 9


def sds(*shape):
    return jax.ShapeDtypeStruct(shape, F32)


def weights(adjoint, bx_minus, bx_here, bx_plus, by, bz, g):
    rows = lax.broadcasted_iota(jnp.int32, (NY, NZ), 0)
    zero = jnp.zeros((NY, NZ), F32)
    here = (1.0 - 6.0 * diffusion) - g
    if adjoint:
        xp, xm = diffusion + bx_plus, diffusion - bx_minus
        yp, ym = diffusion + pltpu.roll(by, NY - 1, 0), diffusion - pltpu.roll(by, 1, 0)
        zp, zm = diffusion + pltpu.roll(bz, NZ - 1, 1), diffusion - pltpu.roll(bz, 1, 1)
    else:
        xp, xm = diffusion - bx_here, diffusion + bx_here
        yp, ym = diffusion - by, diffusion + by
        zp, zm = diffusion - bz, diffusion + bz
    yp = jnp.where(rows == NY - 1, zero, yp)
    ym = jnp.where(rows == 0, zero, ym)
    return here, xp, xm, yp, ym, zp, zm


def apply(w, below, here, above):
    c0, xp, xm, yp, ym, zp, zm = w
    out = c0 * here + xp * above + xm * below
    out = out + yp * pltpu.roll(here, NY - 1, 0) + ym * pltpu.roll(here, 1, 0)
    return out + zp * pltpu.roll(here, NZ - 1, 1) + zm * pltpu.roll(here, 1, 1)


def add_gram(acc, base, fields):
    for p, (i, j) in enumerate(PAIRS):
        prod = fields[i] * fields[j]
        acc[base + p] += (prod[0:8] + prod[8:16]) + (prod[16:24] + prod[24:32])


def pack_kernel(fwd, adj, cf, up, dn, sem):
    copies = []

    def copy(src, dst):
        c = pltpu.make_async_copy(src, dst, sem.at[len(copies)])
        c.start()
        copies.append(c)

    for out, first, inner in ((up, NXL - 3, NXL - 2), (dn, 0, 0)):
        for s, field in enumerate((fwd, adj)):
            for f in range(K):
                copy(field.at[f, pl.ds(first, 3)], out.at[pl.ds((s * K + f) * 3, 3)])
        copy(cf.at[0, pl.ds(first, 3)], out.at[pl.ds(48, 3)])
        for q in range(3):
            copy(cf.at[1 + q, pl.ds(inner, 2)], out.at[pl.ds(51 + 2 * q, 2)])
    for c in copies:
        c.wait()


def pack(fwd, adj, cf):
    vm = pl.BlockSpec(memory_space=pltpu.VMEM)
    return pl.pallas_call(
        pack_kernel,
        out_shape=(sds(PAYLOAD, NY, NZ), sds(PAYLOAD, NY, NZ)),
        in_specs=[ANY, ANY, ANY],
        out_specs=(vm, vm),
        scratch_shapes=[pltpu.SemaphoreType.DMA((40,))],
        name="pack",
    )(fwd, adj, cf)


def interior_kernel(fwd, adj, cf, fout, aout, edge, gram, s1, s2, s3, sem):
    gram[...] = jnp.zeros((2 * NP, 8, NZ), F32)
    for s, src0 in enumerate((fwd, adj)):
        for stage, (lo, hi) in enumerate(((1, 11), (2, 10), (3, 9))):
            src = (src0, s1, s2)[stage]
            base = (0, s * K, s * K)[stage]
            dst = (s1, s2, s3)[stage]

            def body(p, carry, src=src, base=base, dst=dst, s=s):
                w = weights(s == 1, cf[0, p - 1], cf[0, p], cf[0, p + 1], cf[1, p], cf[2, p], cf[3, p])
                for f in range(K):
                    dst[s * K + f, p] = apply(w, src[base + f, p - 1], src[base + f, p], src[base + f, p + 1])
                return carry

            lax.fori_loop(lo, hi, body, 0)

        def body(p, carry, s=s):
            add_gram(gram, s * NP, [s3[s * K + f, p] for f in range(K)])
            return carry

        lax.fori_loop(3, 9, body, 0)
    copies = []
    for s, out in enumerate((fout, aout)):
        copies.append((s3.at[pl.ds(s * K, K), pl.ds(3, 6)], out.at[:, pl.ds(3, 6)]))
    for k, (ref, p) in enumerate(((s1, 1), (s1, 9), (s2, 2), (s2, 8))):
        copies.append((ref.at[:, pl.ds(p, 2)], edge.at[k]))
    copies = [pltpu.make_async_copy(a, b, sem.at[n]) for n, (a, b) in enumerate(copies)]
    for c in copies:
        c.start()
    for c in copies:
        c.wait()


def interior(fwd, adj, cf):
    vm = pl.BlockSpec(memory_space=pltpu.VMEM)
    return pl.pallas_call(
        interior_kernel,
        out_shape=(
            sds(K, NXL, NY, NZ),
            sds(K, NXL, NY, NZ),
            sds(4, 2 * K, 2, NY, NZ),
            sds(2 * NP, 8, NZ),
        ),
        in_specs=[vm, vm, vm],
        out_specs=(ANY, ANY, ANY, vm),
        scratch_shapes=[pltpu.VMEM((2 * K, NXL, NY, NZ), F32)] * 3 + [pltpu.SemaphoreType.DMA((6,))],
        name="interior",
    )(fwd, adj, cf)


def edges_kernel(fwd, adj, cf, fin, ain, edge, gin, up, dn, fout, aout, gout, raw, cw, s1, s2, o, gram, sem):
    del fin, ain
    first, later = [], []

    def copy(src, dst, group):
        c = pltpu.make_async_copy(src, dst, sem.at[len(first) + len(later)])
        c.start()
        group.append(c)

    copy(cf.at[:, pl.ds(0, 4)], cw.at[0, :, pl.ds(3, 4)], first)
    copy(cf.at[:, pl.ds(8, 4)], cw.at[1, :, pl.ds(0, 4)], first)
    copy(up.at[pl.ds(48, 3)], cw.at[0, 0, pl.ds(0, 3)], first)
    copy(dn.at[pl.ds(48, 3)], cw.at[1, 0, pl.ds(4, 3)], first)
    for q in range(3):
        copy(up.at[pl.ds(51 + 2 * q, 2)], cw.at[0, 1 + q, pl.ds(1, 2)], first)
        copy(dn.at[pl.ds(51 + 2 * q, 2)], cw.at[1, 1 + q, pl.ds(4, 2)], first)
    for s, field in enumerate((fwd, adj)):
        rows = pl.ds(s * K, K)
        copy(field.at[:, pl.ds(0, 2)], raw.at[0, rows, pl.ds(3, 2)], first)
        copy(field.at[:, pl.ds(10, 2)], raw.at[1, rows, pl.ds(0, 2)], first)
        for f in range(K):
            n = s * K + f
            copy(up.at[pl.ds(n * 3, 3)], raw.at[0, n, pl.ds(0, 3)], first)
            copy(dn.at[pl.ds(n * 3, 3)], raw.at[1, n, pl.ds(2, 3)], first)
    copy(edge.at[0], s1.at[0, :, pl.ds(3, 2)], later)
    copy(edge.at[1], s1.at[1, :, pl.ds(0, 2)], later)
    copy(edge.at[2], s2.at[0, :, pl.ds(3, 2)], later)
    copy(edge.at[3], s2.at[1, :, pl.ds(0, 2)], later)
    copy(gin, gram, later)
    for c in first:
        c.wait()
    for stage in (1, 2, 3):
        src, dst = ((raw, s1), (s1, s2), (s2, o))[stage - 1]
        for s in range(2):

            def body(t, carry, s=s, stage=stage, src=src, dst=dst):
                side = t // 3
                j = t - side * 3
                center = j + stage + side * (4 - 2 * stage)
                at = j + side * 2 if stage < 3 else j
                w = weights(
                    s == 1,
                    cw[side, 0, center - 1],
                    cw[side, 0, center],
                    cw[side, 0, center + 1],
                    cw[side, 1, center],
                    cw[side, 2, center],
                    cw[side, 3, center],
                )
                for f in range(K):
                    n = s * K + f
                    dst[side, n, at] = apply(w, src[side, n, j], src[side, n, j + 1], src[side, n, j + 2])
                return carry

            lax.fori_loop(0, 6, body, 0)
        if stage == 1:
            for c in later:
                c.wait()
    out = []
    for s, ref in enumerate((fout, aout)):
        for side in range(2):
            c = pltpu.make_async_copy(o.at[side, pl.ds(s * K, K)], ref.at[:, pl.ds(9 * side, 3)], sem.at[len(out)])
            c.start()
            out.append(c)
    for s in range(2):

        def body(t, carry, s=s):
            side = t // 3
            j = t - side * 3
            add_gram(gram, s * NP, [o[side, s * K + f, j] for f in range(K)])
            return carry

        lax.fori_loop(0, 6, body, 0)
    gout[...] = jnp.sum(gram[...], axis=1)
    for c in out:
        c.wait()


def edges(fwd, adj, cf, fin, ain, edge, gram, up, dn):
    vm = pl.BlockSpec(memory_space=pltpu.VMEM)
    return pl.pallas_call(
        edges_kernel,
        out_shape=(sds(K, NXL, NY, NZ), sds(K, NXL, NY, NZ), sds(2 * NP, NZ)),
        in_specs=[ANY] * 9,
        out_specs=(ANY, ANY, vm),
        scratch_shapes=[
            pltpu.VMEM((2, 2 * K, 5, NY, NZ), F32),
            pltpu.VMEM((2, 4, 7, NY, NZ), F32),
            pltpu.VMEM((2, 2 * K, 5, NY, NZ), F32),
            pltpu.VMEM((2, 2 * K, 5, NY, NZ), F32),
            pltpu.VMEM((2, 2 * K, 3, NY, NZ), F32),
            pltpu.VMEM((2 * NP, 8, NZ), F32),
            pltpu.SemaphoreType.DMA((64,)),
        ],
        input_output_aliases={3: 0, 4: 1},
        name="edges",
    )(fwd, adj, cf, fin, ain, edge, gram, up, dn)


def factor(rows):
    row = lax.broadcasted_iota(jnp.int32, (K, NZ), 0)
    lane = lax.broadcasted_iota(jnp.int32, (K, NZ), 1)
    totals = jnp.sum(rows, axis=1, keepdims=True)
    m = jnp.where(lane == row + K, jnp.ones((K, NZ), F32), jnp.zeros((K, NZ), F32))
    for p, (i, j) in enumerate(PAIRS):
        here = ((row == i) & (lane == j)) | ((row == j) & (lane == i))
        m = jnp.where(here, jnp.broadcast_to(totals[p : p + 1], (K, NZ)), m)
    low = jnp.zeros((K, NZ), F32)
    scale = jnp.zeros((K, NZ), F32)
    for k in range(K):
        pivot_row = jnp.broadcast_to(m[k : k + 1, :], (K, NZ))
        column = jnp.broadcast_to(m[:, k : k + 1], (K, NZ))
        pivot = jnp.broadcast_to(pivot_row[:, k : k + 1], (K, NZ))
        root = jnp.sqrt(pivot)
        low = jnp.where((lane == k) & (row >= k), column / root, low)
        scale = jnp.where(row == k, 1.0 / root, scale)
        m = jnp.where(row > k, m - (column / pivot) * pivot_row, m)
    return low, m * scale


def finish_kernel(fin, ain, g, fout, aout, lf, la, coef):
    @pl.when(pl.program_id(0) == 0)
    def _():
        for s, ref in enumerate((lf, la)):
            low, inv = factor(g[pl.ds(s * 40, NP)])
            ref[...] = low
            for p, (i, j) in enumerate(PAIRS):
                coef[s * NP + p] = jnp.broadcast_to(inv[i : i + 1, K + j : K + j + 1], (8, NZ))

    for s, (src, dst) in enumerate(((fin, fout), (ain, aout))):

        def body(p, carry, s=s, src=src, dst=dst):
            fields = [src[f, p] for f in range(K)]
            for i in range(K):
                base = s * NP + i * (i + 1) // 2
                total = coef[base] * fields[0]
                for j in range(1, i + 1):
                    total = total + coef[base + j] * fields[j]
                dst[i, p] = total
            return carry

        lax.fori_loop(0, src.shape[1], body, 0)


def finish(fin, ain, g):
    step = NXL // 4 * 4
    block = pl.BlockSpec((K, step, 8, NZ), lambda c: (0, c, 0, 0))
    small = pl.BlockSpec((K, NZ), lambda c: (0, 0))
    shape = (K, NXL * 4, 8, NZ)
    return pl.pallas_call(
        finish_kernel,
        grid=(4,),
        out_shape=(sds(*shape), sds(*shape), sds(K, NZ), sds(K, NZ)),
        in_specs=[block, block, pl.BlockSpec((80, NZ), lambda c: (0, 0))],
        out_specs=(block, block, small, small),
        scratch_shapes=[pltpu.VMEM((2 * NP, 8, NZ), F32)],
        name="finish",
    )(fin.reshape(shape), ain.reshape(shape), g)


def per_device(forward_sketch, adjoint_sketch, coefficients):
    peers, slices = lax.axis_size("space"), lax.axis_size("tm")
    fwd, adj, cf = forward_sketch[0], adjoint_sketch[0], coefficients[0]
    ring = [(i, (i + 1) % peers) for i in range(peers)]
    back = [(j, i) for i, j in ring]
    later = [(i, (i + 1) % slices) for i in range(slices)]
    earlier = [(j, i) for i, j in later]

    up, dn = pack(fwd, adj, cf)
    up = lax.ppermute(up, "space", ring)
    dn = lax.ppermute(dn, "space", back)
    fpart, apart, edge, gram = interior(fwd, adj, cf)
    fout, aout, gram = edges(fwd, adj, cf, fpart, apart, edge, gram, up, dn)

    fblock = lax.ppermute(fout, "tm", later)
    ablock = lax.ppermute(aout, "tm", earlier)
    hop = 1
    while hop < peers:
        gram = gram + lax.ppermute(gram, "space", [(i, i ^ hop) for i in range(peers)])
        hop *= 2
    gram = gram * (1.0 / (NXL * NY * NZ * peers))
    pad = jnp.zeros((40 - NP, NZ), F32)
    fgram = lax.ppermute(jnp.concatenate([gram[:NP], pad]), "tm", later)
    agram = lax.ppermute(jnp.concatenate([gram[NP:], pad]), "tm", earlier)
    g = jnp.concatenate([fgram, agram])
    fbasis, abasis, flow, alow = finish(fblock, ablock, g)
    shape = (1, K, NXL, NY, NZ)
    return (fbasis.reshape(shape), abasis.reshape(shape), flow[None, :, :K], alow[None, :, :K])


def solution(mesh):
    spec = P("tm", None, "space", None, None)
    return jax.shard_map(
        per_device,
        mesh=mesh,
        in_specs=(spec, spec, spec),
        out_specs=(spec, spec, P("tm", None, None), P("tm", None, None)),
        check_vma=False,
    )
```

```python
import jax
import jax.numpy as jnp
from jax import lax
from jax.experimental import pallas as pl
from jax.experimental.pallas import tpu as pltpu
from jax.sharding import PartitionSpec as P

diffusion = 0.15
K, NXL, NY, NZ = 8, 12, 32, 128
PAD, TALL = 8, 48
PAIRS = [(i, j) for i in range(K) for j in range(i + 1)]
NP = len(PAIRS)
GROWS = 40
F32 = jnp.float32
ANY = pl.BlockSpec(memory_space=pltpu.HBM)
VM = pl.BlockSpec(memory_space=pltpu.VMEM)
PARAMS = pltpu.CompilerParams(vmem_limit_bytes=24 * 1024 * 1024)
COLS = (32, 25)


def sds(*shape):
    return jax.ShapeDtypeStruct(shape, F32)


def vmem(*shape):
    return pltpu.VMEM(shape, F32)


def resident(x):
    return pltpu.with_memory_space_constraint(x, pltpu.VMEM)


def rows(t, dy=0):
    return pl.ds(PAD + 8 * t + dy, 8)


BODY = pl.ds(PAD, NY)


def plane_step(adjoint, coef, src, dst):
    for t in range(NY // 8):
        here = (1.0 - 6.0 * diffusion) - coef(3, 0, rows(t))
        bz = coef(2, 0, rows(t))
        if adjoint:
            xp, xm = diffusion + coef(0, 1, rows(t)), diffusion - coef(0, -1, rows(t))
            yp, ym = diffusion + coef(1, 0, rows(t, 1)), diffusion - coef(1, 0, rows(t, -1))
            zp, zm = diffusion + pltpu.roll(bz, NZ - 1, 1), diffusion - pltpu.roll(bz, 1, 1)
        else:
            bx, by = coef(0, 0, rows(t)), coef(1, 0, rows(t))
            xp, xm = diffusion - bx, diffusion + bx
            yp, ym = diffusion - by, diffusion + by
            zp, zm = diffusion - bz, diffusion + bz
        for f in range(K):
            v = src(f, 0, rows(t))
            x = xp * src(f, 1, rows(t)) + xm * src(f, -1, rows(t))
            y = yp * src(f, 0, rows(t, 1)) + ym * src(f, 0, rows(t, -1))
            z = zp * pltpu.roll(v, NZ - 1, 1) + zm * pltpu.roll(v, 1, 1)
            dst(f, t, (here * v + x) + (y + z))


def add_gram(acc, planes):
    for p, (i, j) in enumerate(PAIRS):
        total = None
        for fields in planes:
            for t in range(NY // 8):
                prod = fields(i, t) * fields(j, t)
                total = prod if total is None else total + prod
        acc[p] += total


def zero_walls(*refs):
    for ref in refs:
        lead = ref.shape[:-2]
        ref[..., pl.ds(0, PAD), :] = jnp.zeros((*lead, PAD, NZ), F32)
        ref[..., pl.ds(PAD + NY, PAD), :] = jnp.zeros((*lead, PAD, NZ), F32)


class Copies:
    def __init__(self, sem):
        self.sem, self.count = sem, 0

    def start(self, src, dst):
        c = pltpu.make_async_copy(src, dst, self.sem.at[self.count])
        self.count += 1
        c.start()
        return c


def wait(copies):
    for c in copies:
        c.wait()


def pack_kernel(fwd, adj, cf, fup, fdn, aup, adn, sem):
    c = Copies(sem)
    work = []
    for fo, ao, first, inner, outer in ((fup, aup, NXL - 3, NXL - 2, NXL - 3), (fdn, adn, 0, 0, 2)):
        for field, out in ((fwd, fo), (adj, ao)):
            for f in range(K):
                work.append(c.start(field.at[f, pl.ds(first, 3)], out.at[pl.ds(f * 3, 3)]))
        for q in range(4):
            work.append(c.start(cf.at[q, pl.ds(inner, 2)], fo.at[pl.ds(24 + 2 * q, 2)]))
        work.append(c.start(cf.at[0, pl.ds(outer, 1)], ao.at[pl.ds(24, 1)]))
    wait(work)


def pack(fwd, adj, cf):
    return pl.pallas_call(
        pack_kernel,
        out_shape=tuple(vmem(n, NY, NZ) for n in (COLS[0], COLS[0], COLS[1], COLS[1])),
        in_specs=[ANY, ANY, ANY],
        out_specs=(VM,) * 4,
        scratch_shapes=[pltpu.SemaphoreType.DMA((42,))],
        compiler_params=PARAMS,
        name="pack",
    )(fwd, adj, cf)


def interior_kernel(fwd, adj, cf, fblock, ablock, fedge, aedge, fgram, agram, fraw, araw, cw, s1, s2, sem):
    c = Copies(sem)
    ready = [
        [c.start(cf, cw.at[:, :, BODY]), c.start(fwd, fraw.at[:, :, BODY])],
        [c.start(adj, araw.at[:, :, BODY])],
    ]
    zero_walls(fraw, araw, cw, s1, s2)
    for s, (raw, block, edge, gram) in enumerate(((fraw, fblock, fedge, fgram), (araw, ablock, aedge, agram))):
        wait(ready[s])
        for stage, (lo, hi) in enumerate(((1, 11), (2, 10), (3, 9))):
            src = (raw, s1, s2)[stage]
            dst = (s1, s2, block)[stage]

            def body(h, carry, s=s, stage=stage, lo=lo, src=src, dst=dst):
                for u in range(2):
                    p = lo + 2 * h + u

                    def put(f, t, value, p=p):
                        if stage < 2:
                            dst[f, p, rows(t)] = value
                        else:
                            dst[f, p, pl.ds(8 * t, 8)] = value

                    plane_step(
                        s == 1,
                        lambda q, dp, r, p=p: cw[q, p + dp, r],
                        lambda f, dp, r, p=p: src[f, p + dp, r],
                        put,
                    )
                return carry

            lax.fori_loop(0, (hi - lo) // 2, body, 0)
        copies = []
        for k, (ref, p) in enumerate(((s1, 1), (s1, 9), (s2, 2), (s2, 8))):
            copies.append(c.start(ref.at[:, pl.ds(p, 2), BODY], edge.at[k]))
        gram[...] = jnp.zeros((NP, 8, NZ), F32)

        def body(h, carry, block=block, gram=gram):
            add_gram(gram, [lambda f, t, p=3 + 2 * h + u: block[f, p, pl.ds(8 * t, 8)] for u in range(2)])
            return carry

        lax.fori_loop(0, 3, body, 0)
        wait(copies)


def interior(fwd, adj, cf):
    tall = pltpu.VMEM((K, NXL, TALL, NZ), F32)
    return pl.pallas_call(
        interior_kernel,
        out_shape=(
            vmem(K, NXL, NY, NZ),
            vmem(K, NXL, NY, NZ),
            vmem(4, K, 2, NY, NZ),
            vmem(4, K, 2, NY, NZ),
            vmem(NP, 8, NZ),
            vmem(NP, 8, NZ),
        ),
        in_specs=[ANY, ANY, ANY],
        out_specs=(VM,) * 6,
        scratch_shapes=[
            tall,
            tall,
            pltpu.VMEM((4, NXL, TALL, NZ), F32),
            tall,
            tall,
            pltpu.SemaphoreType.DMA((16,)),
        ],
        compiler_params=PARAMS,
        name="interior",
    )(fwd, adj, cf)


def edges_kernel(adjoint, *refs):
    if adjoint:
        field, cf, _, edge, gin, cup, cdn, up, dn, block, gout, raw, cw, s1, s2, gram, sem = refs
    else:
        field, cf, _, edge, gin, up, dn, block, gout, raw, cw, s1, s2, gram, sem = refs
        cup, cdn = up, dn
    c = Copies(sem)
    first = [
        c.start(cf.at[:, pl.ds(0, 4)], cw.at[0, :, pl.ds(3, 4), BODY]),
        c.start(cf.at[:, pl.ds(8, 4)], cw.at[1, :, pl.ds(0, 4), BODY]),
        c.start(field.at[:, pl.ds(0, 2)], raw.at[0, :, pl.ds(3, 2), BODY]),
        c.start(field.at[:, pl.ds(10, 2)], raw.at[1, :, pl.ds(0, 2), BODY]),
    ]
    for q in range(4):
        first.append(c.start(cup.at[pl.ds(24 + 2 * q, 2)], cw.at[0, q, pl.ds(1, 2), BODY]))
        first.append(c.start(cdn.at[pl.ds(24 + 2 * q, 2)], cw.at[1, q, pl.ds(4, 2), BODY]))
    if adjoint:
        first.append(c.start(up.at[pl.ds(24, 1)], cw.at[0, 0, pl.ds(0, 1), BODY]))
        first.append(c.start(dn.at[pl.ds(24, 1)], cw.at[1, 0, pl.ds(6, 1), BODY]))
    for f in range(K):
        first.append(c.start(up.at[pl.ds(f * 3, 3)], raw.at[0, f, pl.ds(0, 3), BODY]))
        first.append(c.start(dn.at[pl.ds(f * 3, 3)], raw.at[1, f, pl.ds(2, 3), BODY]))
    later = [
        c.start(edge.at[0], s1.at[0, :, pl.ds(3, 2), BODY]),
        c.start(edge.at[1], s1.at[1, :, pl.ds(0, 2), BODY]),
        c.start(edge.at[2], s2.at[0, :, pl.ds(3, 2), BODY]),
        c.start(edge.at[3], s2.at[1, :, pl.ds(0, 2), BODY]),
    ]
    zero_walls(raw, cw, s1, s2)
    gram[...] = gin[...]
    wait(first)
    for stage in (1, 2, 3):
        src, dst = ((raw, s1), (s1, s2), (s2, block))[stage - 1]

        def body(side, carry, stage=stage, src=src, dst=dst):
            for j in range(3):
                center = j + stage + side * (4 - 2 * stage)

                def put(f, t, value, j=j):
                    if stage < 3:
                        dst[side, f, j + side * 2, rows(t)] = value
                    else:
                        dst[f, j + side * 9, pl.ds(8 * t, 8)] = value

                plane_step(
                    adjoint,
                    lambda q, dp, r, center=center: cw[side, q, center + dp, r],
                    lambda f, dp, r, j=j: src[side, f, j + 1 + dp, r],
                    put,
                )
            return carry

        lax.fori_loop(0, 2, body, 0)
        if stage == 1:
            wait(later)

    def body(side, carry):
        add_gram(gram, [lambda f, t, p=side * 9 + j: block[f, p, pl.ds(8 * t, 8)] for j in range(3)])
        return carry

    lax.fori_loop(0, 2, body, 0)
    gout[pl.ds(0, NP)] = jnp.sum(gram[...], axis=1) * (1.0 / (NXL * NY * NZ * 16))
    gout[pl.ds(NP, GROWS - NP)] = jnp.zeros((GROWS - NP, NZ), F32)


def edges(adjoint, field, cf, block, edge, gram, halos):
    window = pltpu.VMEM((2, K, 5, TALL, NZ), F32)
    return pl.pallas_call(
        lambda *refs: edges_kernel(adjoint, *refs),
        out_shape=(vmem(K, NXL, NY, NZ), vmem(GROWS, NZ)),
        in_specs=[ANY, ANY] + [VM] * (3 + len(halos)),
        out_specs=(VM, VM),
        scratch_shapes=[
            window,
            pltpu.VMEM((2, 4, 7, TALL, NZ), F32),
            window,
            window,
            pltpu.VMEM((NP, 8, NZ), F32),
            pltpu.SemaphoreType.DMA((34,)),
        ],
        input_output_aliases={2: 0},
        compiler_params=PARAMS,
        name="adjoint_edges" if adjoint else "forward_edges",
    )(field, cf, block, edge, gram, *halos)


def finish_kernel(fin, ain, g0, g1, g2, g3, fout, aout, lf, la, gs, coef, fo, ao, sem):
    row = lax.broadcasted_iota(jnp.int32, (K, NZ), 0)
    lane = lax.broadcasted_iota(jnp.int32, (K, NZ), 1)
    gs[0] = jnp.broadcast_to(jnp.sum(g0[...] + g1[...], axis=1, keepdims=True), (GROWS, NZ))
    gs[1] = jnp.broadcast_to(jnp.sum(g2[...] + g3[...], axis=1, keepdims=True), (GROWS, NZ))
    for s, ref in enumerate((lf, la)):
        a = {ij: jnp.broadcast_to(gs[s, p : p + 1, :], (8, NZ)) for p, ij in enumerate(PAIRS)}
        low, diag = {}, []
        for k in range(K):
            root = jnp.sqrt(a[k, k])
            low[k, k] = root
            diag.append(1.0 / root)
            for i in range(k + 1, K):
                low[i, k] = a[i, k] * diag[k]
            for i in range(k + 1, K):
                for j in range(k + 1, i + 1):
                    a[i, j] = a[i, j] - low[i, k] * low[j, k]
        matrix = jnp.zeros((K, NZ), F32)
        for i, j in PAIRS:
            matrix = jnp.where((row == i) & (lane == j), low[i, j], matrix)
        ref[...] = matrix[:, :K]
        inv = {}
        for j in range(K):
            inv[j, j] = diag[j]
            for i in range(j + 1, K):
                total = low[i, j] * inv[j, j]
                for m in range(j + 1, i):
                    total = total + low[i, m] * inv[m, j]
                inv[i, j] = -total * diag[i]
        for p, ij in enumerate(PAIRS):
            coef[s * NP + p] = inv[ij]
    c = Copies(sem)
    work = []
    for s, (src, dst, out) in enumerate(((fin, fo, fout), (ain, ao, aout))):
        for part in range(3):

            def body(p, carry, s=s, src=src, dst=dst):
                for t in range(NY // 8):
                    fields = [src[f, p, pl.ds(8 * t, 8)] for f in range(K)]
                    for i in range(K):
                        base = s * NP + i * (i + 1) // 2
                        total = coef[base] * fields[0]
                        for j in range(1, i + 1):
                            total = total + coef[base + j] * fields[j]
                        dst[i, p, pl.ds(8 * t, 8)] = total
                return carry

            lax.fori_loop(4 * part, 4 * part + 4, body, 0)
            planes = pl.ds(4 * part, 4)
            work.append(c.start(dst.at[:, planes], out.at[:, planes]))
    wait(work)


def finish(fin, ain, grams):
    block = pltpu.VMEM((K, NXL, NY, NZ), F32)
    shape = sds(K, NXL, NY, NZ)
    return pl.pallas_call(
        finish_kernel,
        out_shape=(shape, shape, sds(K, K), sds(K, K)),
        in_specs=[VM] * 6,
        out_specs=(ANY, ANY, VM, VM),
        scratch_shapes=[
            pltpu.VMEM((2, GROWS, NZ), F32),
            pltpu.VMEM((2 * NP, 8, NZ), F32),
            block,
            block,
            pltpu.SemaphoreType.DMA((6,)),
        ],
        compiler_params=PARAMS,
        name="finish",
    )(fin, ain, *grams)


def per_device(forward_sketch, adjoint_sketch, coefficients):
    peers, slices = lax.axis_size("space"), lax.axis_size("tm")
    fwd, adj, cf = forward_sketch[0], adjoint_sketch[0], coefficients[0]
    ring = [(i, (i + 1) % peers) for i in range(peers)]
    back = [(j, i) for i, j in ring]
    later = [(i, (i + 1) % slices) for i in range(slices)]
    earlier = [(j, i) for i, j in later]

    def hop(by, flip):
        return [
            (t * peers + s, ((t + by) % slices) * peers + (s ^ flip)) for t in range(slices) for s in range(peers)
        ]

    fup, fdn, aup, adn = pack(fwd, adj, cf)
    fup, fdn = lax.ppermute(fup, "space", ring), lax.ppermute(fdn, "space", back)
    aup, adn = lax.ppermute(aup, "space", ring), lax.ppermute(adn, "space", back)
    fup, fdn, aup, adn = resident(fup), resident(fdn), resident(aup), resident(adn)
    fblock, ablock, fedge, aedge, fgram, agram = interior(fwd, adj, cf)
    fblock, fgram = edges(False, fwd, cf, fblock, fedge, fgram, (fup, fdn))
    ablock, agram = edges(True, adj, cf, ablock, aedge, agram, (fup, fdn, aup, adn))

    fblock = lax.ppermute(fblock, "tm", later)
    ablock = lax.ppermute(ablock, "tm", earlier)
    gram = jnp.concatenate([fgram, agram])
    for d in (1, 2, 4):
        gram = gram + lax.ppermute(gram, "space", [(i, i ^ d) for i in range(peers)])
    grams = [
        lax.ppermute(half, ("tm", "space"), hop(by, flip))
        for half, by in ((gram[:GROWS], 1), (gram[GROWS:], -1))
        for flip in (0, 8)
    ]
    outs = finish(resident(fblock), resident(ablock), [resident(g) for g in grams])
    return tuple(o[None] for o in outs)


def solution(mesh):
    spec = P("tm", None, "space", None, None)
    return jax.shard_map(
        per_device,
        mesh=mesh,
        in_specs=(spec, spec, spec),
        out_specs=(spec, spec, P("tm", None, None), P("tm", None, None)),
        check_vma=False,
    )
```

```python
import jax
import jax.numpy as jnp
from jax import lax
from jax.experimental import pallas as pl
from jax.experimental.pallas import tpu as pltpu
from jax.sharding import PartitionSpec as P

diffusion = 0.15
K, NXL, NY, NZ = 8, 12, 32, 128
PAD, TALL = 8, 48
PAIRS = [(i, j) for i in range(K) for j in range(i + 1)]
NP = len(PAIRS)
GROWS = 40
F32 = jnp.float32
ANY = pl.BlockSpec(memory_space=pltpu.HBM)
VM = pl.BlockSpec(memory_space=pltpu.VMEM)
PARAMS = pltpu.CompilerParams(vmem_limit_bytes=24 * 1024 * 1024)


def sds(*shape):
    return jax.ShapeDtypeStruct(shape, F32)


def vmem(*shape):
    return pltpu.VMEM(shape, F32)


def resident(x):
    return pltpu.with_memory_space_constraint(x, pltpu.VMEM)


def rows(t, dy=0):
    return pl.ds(PAD + 8 * t + dy, 8)


BODY = pl.ds(PAD, NY)


def plane_step(adjoint, coef, src, dst):
    for t in range(NY // 8):
        here = (1.0 - 6.0 * diffusion) - coef(3, 0, rows(t))
        bz = coef(2, 0, rows(t))
        if adjoint:
            xp, xm = diffusion + coef(0, 1, rows(t)), diffusion - coef(0, -1, rows(t))
            yp, ym = diffusion + coef(1, 0, rows(t, 1)), diffusion - coef(1, 0, rows(t, -1))
            zp, zm = diffusion + pltpu.roll(bz, NZ - 1, 1), diffusion - pltpu.roll(bz, 1, 1)
        else:
            bx, by = coef(0, 0, rows(t)), coef(1, 0, rows(t))
            xp, xm = diffusion - bx, diffusion + bx
            yp, ym = diffusion - by, diffusion + by
            zp, zm = diffusion - bz, diffusion + bz
        for f in range(K):
            v = src(f, 0, rows(t))
            x = xp * src(f, 1, rows(t)) + xm * src(f, -1, rows(t))
            y = yp * src(f, 0, rows(t, 1)) + ym * src(f, 0, rows(t, -1))
            z = zp * pltpu.roll(v, NZ - 1, 1) + zm * pltpu.roll(v, 1, 1)
            dst(f, t, (here * v + x) + (y + z))


def add_gram(acc, planes):
    for p, (i, j) in enumerate(PAIRS):
        total = None
        for fields in planes:
            for t in range(NY // 8):
                prod = fields(i, t) * fields(j, t)
                total = prod if total is None else total + prod
        acc[p] += total


def zero_walls(*refs):
    for ref in refs:
        lead = ref.shape[:-2]
        ref[..., pl.ds(0, PAD), :] = jnp.zeros((*lead, PAD, NZ), F32)
        ref[..., pl.ds(PAD + NY, PAD), :] = jnp.zeros((*lead, PAD, NZ), F32)


class Copies:
    def __init__(self, sem):
        self.sem, self.count = sem, 0

    def start(self, src, dst):
        c = pltpu.make_async_copy(src, dst, self.sem.at[self.count])
        self.count += 1
        c.start()
        return c


def wait(copies):
    for c in copies:
        c.wait()


def parity():
    return lax.axis_index("space") % 2


def pack_kernel(adjoint, field, cf, *refs):
    *outs, raw, cw, sem = refs
    c = Copies(sem)
    loads, sends = [], []
    to_next = [parity(), 1 - parity()]
    for k, out in enumerate(outs):
        first, inner, outer = (to_next[k] * (NXL - n) for n in (3, 2, 1))
        loads.append(c.start(field.at[:, pl.ds(first, 3)], raw.at[k, :, :, BODY]))
        loads.append(c.start(cf.at[:, pl.ds(first, 3)], cw.at[k, :, :, BODY]))
        sends.append(c.start(field.at[:, pl.ds(inner, 2)], out.at[pl.ds(0, K), pl.ds(to_next[k], 2)]))
        if out.shape[0] > K:
            sends.append(c.start(cf.at[0, pl.ds(inner, 2)], out.at[K, pl.ds(0, 2)]))
            sends.append(c.start(cf.at[1, outer], out.at[K, 2]))
            sends.append(c.start(cf.at[2, outer], out.at[K + 1, 0]))
            sends.append(c.start(cf.at[3, outer], out.at[K + 1, 1]))
    for ref, n in ((raw, K), (cw, 4)):
        for row in (0, PAD + NY):
            ref[:, :, pl.ds(1, 1), pl.ds(row, PAD), :] = jnp.zeros((2, n, 1, PAD, NZ), F32)
    wait(loads)
    for k, out in enumerate(outs):
        slot = 2 - 2 * to_next[k]

        def put(f, t, value, out=out, slot=slot):
            out[f, slot, pl.ds(8 * t, 8)] = value

        plane_step(
            adjoint,
            lambda q, dp, r, k=k: cw[k, q, 1 + dp, r],
            lambda f, dp, r, k=k: raw[k, f, 1 + dp, r],
            put,
        )
    wait(sends)


def pack(adjoint, field, cf):
    out = vmem(K if adjoint else K + 2, 3, NY, NZ)
    return pl.pallas_call(
        lambda *refs: pack_kernel(adjoint, *refs),
        out_shape=(out, out),
        in_specs=[ANY, ANY],
        out_specs=(VM, VM),
        scratch_shapes=[
            pltpu.VMEM((2, K, 3, TALL, NZ), F32),
            pltpu.VMEM((2, 4, 3, TALL, NZ), F32),
            pltpu.SemaphoreType.DMA((16,)),
        ],
        compiler_params=PARAMS,
        name="adjoint_pack" if adjoint else "forward_pack",
    )(field, cf)


def interior_kernel(fwd, adj, cf, fblock, ablock, fedge, aedge, fgram, agram, fraw, araw, cw, s1, s2, sem):
    c = Copies(sem)
    ready = [
        [c.start(cf, cw.at[:, :, BODY]), c.start(fwd, fraw.at[:, :, BODY])],
        [c.start(adj, araw.at[:, :, BODY])],
    ]
    zero_walls(fraw, araw, cw, s1, s2)
    for s, (raw, block, edge, gram) in enumerate(((fraw, fblock, fedge, fgram), (araw, ablock, aedge, agram))):
        wait(ready[s])
        for stage, (lo, hi) in enumerate(((1, 11), (2, 10), (3, 9))):
            src = (raw, s1, s2)[stage]
            dst = (s1, s2, block)[stage]

            def body(h, carry, s=s, stage=stage, lo=lo, src=src, dst=dst):
                for u in range(2):
                    p = lo + 2 * h + u

                    def put(f, t, value, p=p):
                        if stage < 2:
                            dst[f, p, rows(t)] = value
                        else:
                            dst[f, p, pl.ds(8 * t, 8)] = value

                    plane_step(
                        s == 1,
                        lambda q, dp, r, p=p: cw[q, p + dp, r],
                        lambda f, dp, r, p=p: src[f, p + dp, r],
                        put,
                    )
                return carry

            lax.fori_loop(0, (hi - lo) // 2, body, 0)
        copies = []
        for k, (ref, p) in enumerate(((s1, 1), (s1, 9), (s2, 2), (s2, 8))):
            copies.append(c.start(ref.at[:, pl.ds(p, 2), BODY], edge.at[k]))
        gram[...] = jnp.zeros((NP, 8, NZ), F32)

        def body(h, carry, block=block, gram=gram):
            add_gram(gram, [lambda f, t, p=3 + 2 * h + u: block[f, p, pl.ds(8 * t, 8)] for u in range(2)])
            return carry

        lax.fori_loop(0, 3, body, 0)
        wait(copies)


def interior(fwd, adj, cf):
    tall = pltpu.VMEM((K, NXL, TALL, NZ), F32)
    return pl.pallas_call(
        interior_kernel,
        out_shape=(
            vmem(K, NXL, NY, NZ),
            vmem(K, NXL, NY, NZ),
            vmem(4, K, 2, NY, NZ),
            vmem(4, K, 2, NY, NZ),
            vmem(NP, 8, NZ),
            vmem(NP, 8, NZ),
        ),
        in_specs=[ANY, ANY, ANY],
        out_specs=(VM,) * 6,
        scratch_shapes=[
            tall,
            tall,
            pltpu.VMEM((4, NXL, TALL, NZ), F32),
            tall,
            tall,
            pltpu.SemaphoreType.DMA((16,)),
        ],
        compiler_params=PARAMS,
        name="interior",
    )(fwd, adj, cf)


def edges_kernel(adjoint, *refs):
    if adjoint:
        field, cf, _, edge, gin, *halos = refs[:9]
    else:
        field, cf, _, edge, gin, *halos = refs[:7]
    block, gout, raw, cw, s1, s2, gram, sem = refs[len(refs) - 8 :]
    c = Copies(sem)
    first = [
        c.start(cf.at[:, pl.ds(0, 4)], cw.at[0, :, pl.ds(3, 4), BODY]),
        c.start(cf.at[:, pl.ds(8, 4)], cw.at[1, :, pl.ds(0, 4), BODY]),
        c.start(field.at[:, pl.ds(0, 2)], raw.at[0, :, pl.ds(3, 2), BODY]),
        c.start(field.at[:, pl.ds(10, 2)], raw.at[1, :, pl.ds(0, 2), BODY]),
    ]
    for k in range(2):
        side = parity() if k == 0 else 1 - parity()
        shared, own = halos[k], halos[len(halos) - 2 + k]
        first.append(c.start(own.at[pl.ds(0, K), pl.ds(1 - side, 2)], raw.at[side, :, pl.ds(1 + side, 2), BODY]))
        first.append(c.start(own.at[pl.ds(0, K), pl.ds(2 * side, 1)], s1.at[side, :, pl.ds(4 * side, 1), BODY]))
        first.append(c.start(shared.at[K, pl.ds(0, 2)], cw.at[side, 0, pl.ds(1 + 3 * side, 2), BODY]))
        for q, at in enumerate(((K, 2), (K + 1, 0), (K + 1, 1))):
            first.append(c.start(shared.at[at], cw.at[side, 1 + q, 2 + 2 * side, BODY]))
    later = [
        c.start(edge.at[0], s1.at[0, :, pl.ds(3, 2), BODY]),
        c.start(edge.at[1], s1.at[1, :, pl.ds(0, 2), BODY]),
        c.start(edge.at[2], s2.at[0, :, pl.ds(3, 2), BODY]),
        c.start(edge.at[3], s2.at[1, :, pl.ds(0, 2), BODY]),
    ]
    zero_walls(raw, cw, s1, s2)
    gram[...] = gin[...]
    wait(first)
    for stage in (1, 2, 3):
        src, dst = ((raw, s1), (s1, s2), (s2, block))[stage - 1]

        def body(side, carry, stage=stage, src=src, dst=dst):
            for u in range(2 if stage == 1 else 3):
                j = u + 1 - side if stage == 1 else u
                center = j + stage + side * (4 - 2 * stage)

                def put(f, t, value, j=j):
                    if stage < 3:
                        dst[side, f, j + side * 2, rows(t)] = value
                    else:
                        dst[f, j + side * 9, pl.ds(8 * t, 8)] = value

                plane_step(
                    adjoint,
                    lambda q, dp, r, center=center: cw[side, q, center + dp, r],
                    lambda f, dp, r, j=j: src[side, f, j + 1 + dp, r],
                    put,
                )
            return carry

        lax.fori_loop(0, 2, body, 0)
        if stage == 1:
            wait(later)

    def body(side, carry):
        add_gram(gram, [lambda f, t, p=side * 9 + j: block[f, p, pl.ds(8 * t, 8)] for j in range(3)])
        return carry

    lax.fori_loop(0, 2, body, 0)
    gout[pl.ds(0, NP)] = jnp.sum(gram[...], axis=1) * (1.0 / (NXL * NY * NZ * 16))
    gout[pl.ds(NP, GROWS - NP)] = jnp.zeros((GROWS - NP, NZ), F32)


def edges(adjoint, field, cf, block, edge, gram, halos):
    window = pltpu.VMEM((2, K, 5, TALL, NZ), F32)
    return pl.pallas_call(
        lambda *refs: edges_kernel(adjoint, *refs),
        out_shape=(vmem(K, NXL, NY, NZ), vmem(GROWS, NZ)),
        in_specs=[ANY, ANY] + [VM] * (3 + len(halos)),
        out_specs=(VM, VM),
        scratch_shapes=[
            window,
            pltpu.VMEM((2, 4, 7, TALL, NZ), F32),
            window,
            window,
            pltpu.VMEM((NP, 8, NZ), F32),
            pltpu.SemaphoreType.DMA((24,)),
        ],
        input_output_aliases={2: 0},
        compiler_params=PARAMS,
        name="adjoint_edges" if adjoint else "forward_edges",
    )(field, cf, block, edge, gram, *halos)


def finish_kernel(fin, ain, gf, g0, g1, fout, aout, lf, la, gs, coef, fo, ao, sem):
    row = lax.broadcasted_iota(jnp.int32, (K, NZ), 0)
    lane = lax.broadcasted_iota(jnp.int32, (K, NZ), 1)
    ga = g0[pl.ds(GROWS, GROWS)] + g1[pl.ds(GROWS, GROWS)]
    gs[0] = jnp.broadcast_to(jnp.sum(gf[pl.ds(0, GROWS)], axis=1, keepdims=True), (GROWS, NZ))
    gs[1] = jnp.broadcast_to(jnp.sum(ga, axis=1, keepdims=True), (GROWS, NZ))
    for s, ref in enumerate((lf, la)):
        a = {ij: jnp.broadcast_to(gs[s, p : p + 1, :], (8, NZ)) for p, ij in enumerate(PAIRS)}
        low, diag = {}, []
        for k in range(K):
            root = jnp.sqrt(a[k, k])
            low[k, k] = root
            diag.append(1.0 / root)
            for i in range(k + 1, K):
                low[i, k] = a[i, k] * diag[k]
            for i in range(k + 1, K):
                for j in range(k + 1, i + 1):
                    a[i, j] = a[i, j] - low[i, k] * low[j, k]
        matrix = jnp.zeros((K, NZ), F32)
        for i, j in PAIRS:
            matrix = jnp.where((row == i) & (lane == j), low[i, j], matrix)
        ref[...] = matrix[:, :K]
        inv = {}
        for j in range(K):
            inv[j, j] = diag[j]
            for i in range(j + 1, K):
                total = low[i, j] * inv[j, j]
                for m in range(j + 1, i):
                    total = total + low[i, m] * inv[m, j]
                inv[i, j] = -total * diag[i]
        for p, ij in enumerate(PAIRS):
            coef[s * NP + p] = inv[ij]
    c = Copies(sem)
    work = []
    for s, (src, dst, out) in enumerate(((fin, fo, fout), (ain, ao, aout))):
        for part in range(3):

            def body(p, carry, s=s, src=src, dst=dst):
                for t in range(NY // 8):
                    fields = [src[f, p, pl.ds(8 * t, 8)] for f in range(K)]
                    for i in range(K):
                        base = s * NP + i * (i + 1) // 2
                        total = coef[base] * fields[0]
                        for j in range(1, i + 1):
                            total = total + coef[base + j] * fields[j]
                        dst[i, p, pl.ds(8 * t, 8)] = total
                return carry

            lax.fori_loop(4 * part, 4 * part + 4, body, 0)
            planes = pl.ds(4 * part, 4)
            work.append(c.start(dst.at[:, planes], out.at[:, planes]))
    wait(work)


def finish(fin, ain, grams):
    block = pltpu.VMEM((K, NXL, NY, NZ), F32)
    shape = sds(K, NXL, NY, NZ)
    return pl.pallas_call(
        finish_kernel,
        out_shape=(shape, shape, sds(K, K), sds(K, K)),
        in_specs=[VM] * 5,
        out_specs=(ANY, ANY, VM, VM),
        scratch_shapes=[
            pltpu.VMEM((2, GROWS, NZ), F32),
            pltpu.VMEM((2 * NP, 8, NZ), F32),
            block,
            block,
            pltpu.SemaphoreType.DMA((6,)),
        ],
        compiler_params=PARAMS,
        name="finish",
    )(fin, ain, *grams)


def per_device(forward_sketch, adjoint_sketch, coefficients):
    peers, slices = lax.axis_size("space"), lax.axis_size("tm")
    fwd, adj, cf = (pltpu.with_memory_space_constraint(x[0], pltpu.HBM) for x in (forward_sketch, adjoint_sketch, coefficients))
    partner = [
        [(i, (i + 1 if (i % 2 == 1) == (k == 0) else i - 1) % peers) for i in range(peers)] for k in range(2)
    ]
    later = [(i, (i + 1) % slices) for i in range(slices)]
    earlier = [(j, i) for i, j in later]

    def hop(by, flip):
        return [
            (t * peers + s, ((t + by) % slices) * peers + (s ^ flip)) for t in range(slices) for s in range(peers)
        ]

    fhalo = [lax.ppermute(x, "space", partner[k]) for k, x in enumerate(pack(False, fwd, cf))]
    ahalo = [lax.ppermute(x, "space", partner[k]) for k, x in enumerate(pack(True, adj, cf))]
    fhalo, ahalo = [resident(x) for x in fhalo], [resident(x) for x in ahalo]
    fblock, ablock, fedge, aedge, fgram, agram = interior(fwd, adj, cf)
    fblock, fgram = edges(False, fwd, cf, fblock, fedge, fgram, fhalo)
    fgram = sum(lax.ppermute(fgram, ("tm", "space"), hop(1, flip)) for flip in (0, 8))
    ablock, agram = edges(True, adj, cf, ablock, aedge, agram, fhalo + ahalo)
    fblock = lax.ppermute(fblock, "tm", later)
    ablock = lax.ppermute(ablock, "tm", earlier)
    gram = jnp.concatenate([fgram, agram])
    for d in (1, 2, 7):
        gram = gram + lax.ppermute(gram, "space", [(i, i ^ d) for i in range(peers)])
    grams = [gram] + [lax.ppermute(gram, ("tm", "space"), hop(-1, flip)) for flip in (0, 8)]
    outs = finish(resident(fblock), resident(ablock), [resident(g) for g in grams])
    return tuple(o[None] for o in outs)


def solution(mesh):
    spec = P("tm", None, "space", None, None)
    return jax.shard_map(
        per_device,
        mesh=mesh,
        in_specs=(spec, spec, spec),
        out_specs=(spec, spec, P("tm", None, None), P("tm", None, None)),
        check_vma=False,
    )
```

```python
import jax
import jax.numpy as jnp
from jax import lax
from jax.experimental import pallas as pl
from jax.experimental.pallas import tpu as pltpu
from jax.sharding import PartitionSpec as P

diffusion = 0.15
K, NXL, NY, NZ = 8, 12, 32, 128
PAD, TALL = 8, 48
PAIRS = [(i, j) for i in range(K) for j in range(i + 1)]
NP = len(PAIRS)
GROWS = 40
F32 = jnp.float32
ANY = pl.BlockSpec(memory_space=pltpu.HBM)
VM = pl.BlockSpec(memory_space=pltpu.VMEM)
PARAMS = pltpu.CompilerParams(vmem_limit_bytes=24 * 1024 * 1024)


def sds(*shape):
    return jax.ShapeDtypeStruct(shape, F32)


def vmem(*shape):
    return pltpu.VMEM(shape, F32)


def resident(x):
    return pltpu.with_memory_space_constraint(x, pltpu.VMEM)


def rows(t, dy=0):
    return pl.ds(PAD + 8 * t + dy, 8)


BODY = pl.ds(PAD, NY)


def plane_step(adjoint, coef, src, dst):
    for t in range(NY // 8):
        here = (1.0 - 6.0 * diffusion) - coef(3, 0, rows(t))
        bz = coef(2, 0, rows(t))
        if adjoint:
            xp, xm = diffusion + coef(0, 1, rows(t)), diffusion - coef(0, -1, rows(t))
            yp, ym = diffusion + coef(1, 0, rows(t, 1)), diffusion - coef(1, 0, rows(t, -1))
            zp, zm = diffusion + pltpu.roll(bz, NZ - 1, 1), diffusion - pltpu.roll(bz, 1, 1)
        else:
            bx, by = coef(0, 0, rows(t)), coef(1, 0, rows(t))
            xp, xm = diffusion - bx, diffusion + bx
            yp, ym = diffusion - by, diffusion + by
            zp, zm = diffusion - bz, diffusion + bz
        for f in range(K):
            v = src(f, 0, rows(t))
            x = xp * src(f, 1, rows(t)) + xm * src(f, -1, rows(t))
            y = yp * src(f, 0, rows(t, 1)) + ym * src(f, 0, rows(t, -1))
            z = zp * pltpu.roll(v, NZ - 1, 1) + zm * pltpu.roll(v, 1, 1)
            dst(f, t, (here * v + x) + (y + z))


def add_gram(acc, planes):
    for p, (i, j) in enumerate(PAIRS):
        total = None
        for fields in planes:
            for t in range(NY // 8):
                prod = fields(i, t) * fields(j, t)
                total = prod if total is None else total + prod
        acc[p] += total


def zero_walls(*refs):
    for ref in refs:
        lead = ref.shape[:-2]
        ref[..., pl.ds(0, PAD), :] = jnp.zeros((*lead, PAD, NZ), F32)
        ref[..., pl.ds(PAD + NY, PAD), :] = jnp.zeros((*lead, PAD, NZ), F32)


class Copies:
    def __init__(self, sem):
        self.sem, self.count = sem, 0

    def start(self, src, dst):
        c = pltpu.make_async_copy(src, dst, self.sem.at[self.count])
        self.count += 1
        c.start()
        return c


def wait(copies):
    for c in copies:
        c.wait()


def parity():
    return lax.axis_index("space") % 2


def pack_kernel(adjoint, field, cf, *refs):
    *outs, raw, cw, sem = refs
    c = Copies(sem)
    loads, sends = [], []
    to_next = [parity(), 1 - parity()]
    for k, out in enumerate(outs):
        first, inner, outer = (to_next[k] * (NXL - n) for n in (3, 2, 1))
        loads.append(c.start(field.at[:, pl.ds(first, 3)], raw.at[k, :, :, BODY]))
        loads.append(c.start(cf.at[:, pl.ds(first, 3)], cw.at[k, :, :, BODY]))
        sends.append(c.start(field.at[:, pl.ds(inner, 2)], out.at[pl.ds(0, K), pl.ds(to_next[k], 2)]))
        if out.shape[0] > K:
            sends.append(c.start(cf.at[0, pl.ds(inner, 2)], out.at[K, pl.ds(0, 2)]))
            sends.append(c.start(cf.at[1, outer], out.at[K, 2]))
            sends.append(c.start(cf.at[2, outer], out.at[K + 1, 0]))
            sends.append(c.start(cf.at[3, outer], out.at[K + 1, 1]))
    for ref, n in ((raw, K), (cw, 4)):
        for row in (0, PAD + NY):
            ref[:, :, pl.ds(1, 1), pl.ds(row, PAD), :] = jnp.zeros((2, n, 1, PAD, NZ), F32)
    wait(loads)
    for k, out in enumerate(outs):
        slot = 2 - 2 * to_next[k]

        def put(f, t, value, out=out, slot=slot):
            out[f, slot, pl.ds(8 * t, 8)] = value

        plane_step(
            adjoint,
            lambda q, dp, r, k=k: cw[k, q, 1 + dp, r],
            lambda f, dp, r, k=k: raw[k, f, 1 + dp, r],
            put,
        )
    wait(sends)


def pack(adjoint, field, cf):
    out = vmem(K if adjoint else K + 2, 3, NY, NZ)
    return pl.pallas_call(
        lambda *refs: pack_kernel(adjoint, *refs),
        out_shape=(out, out),
        in_specs=[ANY, ANY],
        out_specs=(VM, VM),
        scratch_shapes=[
            pltpu.VMEM((2, K, 3, TALL, NZ), F32),
            pltpu.VMEM((2, 4, 3, TALL, NZ), F32),
            pltpu.SemaphoreType.DMA((16,)),
        ],
        compiler_params=PARAMS,
        name="adjoint_pack" if adjoint else "forward_pack",
    )(field, cf)


def interior_kernel(fwd, adj, cf, fblock, ablock, fedge, aedge, fgram, agram, fraw, araw, cw, s1, s2, sem):
    c = Copies(sem)
    ready = [
        [c.start(cf, cw.at[:, :, BODY]), c.start(fwd, fraw.at[:, :, BODY])],
        [c.start(adj, araw.at[:, :, BODY])],
    ]
    zero_walls(fraw, araw, cw, s1, s2)
    for s, (raw, block, edge, gram) in enumerate(((fraw, fblock, fedge, fgram), (araw, ablock, aedge, agram))):
        wait(ready[s])
        for stage, (lo, hi) in enumerate(((1, 11), (2, 10), (3, 9))):
            src = (raw, s1, s2)[stage]
            dst = (s1, s2, block)[stage]

            def body(h, carry, s=s, stage=stage, lo=lo, src=src, dst=dst):
                for u in range(2):
                    p = lo + 2 * h + u

                    def put(f, t, value, p=p):
                        if stage < 2:
                            dst[f, p, rows(t)] = value
                        else:
                            dst[f, p, pl.ds(8 * t, 8)] = value

                    plane_step(
                        s == 1,
                        lambda q, dp, r, p=p: cw[q, p + dp, r],
                        lambda f, dp, r, p=p: src[f, p + dp, r],
                        put,
                    )
                return carry

            lax.fori_loop(0, (hi - lo) // 2, body, 0)
        copies = []
        for k, (ref, p) in enumerate(((s1, 1), (s1, 9), (s2, 2), (s2, 8))):
            copies.append(c.start(ref.at[:, pl.ds(p, 2), BODY], edge.at[k]))
        gram[...] = jnp.zeros((NP, 8, NZ), F32)

        def body(h, carry, block=block, gram=gram):
            add_gram(gram, [lambda f, t, p=3 + 2 * h + u: block[f, p, pl.ds(8 * t, 8)] for u in range(2)])
            return carry

        lax.fori_loop(0, 3, body, 0)
        wait(copies)


def interior(fwd, adj, cf):
    tall = pltpu.VMEM((K, NXL, TALL, NZ), F32)
    return pl.pallas_call(
        interior_kernel,
        out_shape=(
            vmem(K, NXL, NY, NZ),
            vmem(K, NXL, NY, NZ),
            vmem(4, K, 2, NY, NZ),
            vmem(4, K, 2, NY, NZ),
            vmem(NP, 8, NZ),
            vmem(NP, 8, NZ),
        ),
        in_specs=[ANY, ANY, ANY],
        out_specs=(VM,) * 6,
        scratch_shapes=[
            tall,
            tall,
            pltpu.VMEM((4, NXL, TALL, NZ), F32),
            tall,
            tall,
            pltpu.SemaphoreType.DMA((16,)),
        ],
        compiler_params=PARAMS,
        name="interior",
    )(fwd, adj, cf)


def edges_kernel(adjoint, *refs):
    if adjoint:
        field, cf, _, edge, gin, *halos = refs[:9]
    else:
        field, cf, _, edge, gin, *halos = refs[:7]
    block, gout, raw, cw, s1, s2, gram, sem = refs[len(refs) - 8 :]
    c = Copies(sem)
    first = [
        c.start(cf.at[:, pl.ds(0, 4)], cw.at[0, :, pl.ds(3, 4), BODY]),
        c.start(cf.at[:, pl.ds(8, 4)], cw.at[1, :, pl.ds(0, 4), BODY]),
        c.start(field.at[:, pl.ds(0, 2)], raw.at[0, :, pl.ds(3, 2), BODY]),
        c.start(field.at[:, pl.ds(10, 2)], raw.at[1, :, pl.ds(0, 2), BODY]),
    ]
    for k in range(2):
        side = parity() if k == 0 else 1 - parity()
        shared, own = halos[k], halos[len(halos) - 2 + k]
        first.append(c.start(own.at[pl.ds(0, K), pl.ds(1 - side, 2)], raw.at[side, :, pl.ds(1 + side, 2), BODY]))
        first.append(c.start(own.at[pl.ds(0, K), pl.ds(2 * side, 1)], s1.at[side, :, pl.ds(4 * side, 1), BODY]))
        first.append(c.start(shared.at[K, pl.ds(0, 2)], cw.at[side, 0, pl.ds(1 + 3 * side, 2), BODY]))
        for q, at in enumerate(((K, 2), (K + 1, 0), (K + 1, 1))):
            first.append(c.start(shared.at[at], cw.at[side, 1 + q, 2 + 2 * side, BODY]))
    later = [
        c.start(edge.at[0], s1.at[0, :, pl.ds(3, 2), BODY]),
        c.start(edge.at[1], s1.at[1, :, pl.ds(0, 2), BODY]),
        c.start(edge.at[2], s2.at[0, :, pl.ds(3, 2), BODY]),
        c.start(edge.at[3], s2.at[1, :, pl.ds(0, 2), BODY]),
    ]
    zero_walls(raw, cw, s1, s2)
    gram[...] = gin[...]
    wait(first)
    for stage in (1, 2, 3):
        src, dst = ((raw, s1), (s1, s2), (s2, block))[stage - 1]

        def body(side, carry, stage=stage, src=src, dst=dst):
            for u in range(2 if stage == 1 else 3):
                j = u + 1 - side if stage == 1 else u
                center = j + stage + side * (4 - 2 * stage)

                def put(f, t, value, j=j):
                    if stage < 3:
                        dst[side, f, j + side * 2, rows(t)] = value
                    else:
                        dst[f, j + side * 9, pl.ds(8 * t, 8)] = value

                plane_step(
                    adjoint,
                    lambda q, dp, r, center=center: cw[side, q, center + dp, r],
                    lambda f, dp, r, j=j: src[side, f, j + 1 + dp, r],
                    put,
                )
            return carry

        for side in range(2):
            body(side, 0)
        if stage == 1:
            wait(later)

    for side in range(2):
        base = side * (NXL - 3)
        add_gram(gram, [lambda f, t, p=base + j: block[f, p, pl.ds(8 * t, 8)] for j in range(3)])
    gout[pl.ds(0, NP)] = jnp.sum(gram[...], axis=1) * (1.0 / (NXL * NY * NZ * 16))
    gout[pl.ds(NP, GROWS - NP)] = jnp.zeros((GROWS - NP, NZ), F32)


def edges(adjoint, field, cf, block, edge, gram, halos):
    window = pltpu.VMEM((2, K, 5, TALL, NZ), F32)
    return pl.pallas_call(
        lambda *refs: edges_kernel(adjoint, *refs),
        out_shape=(vmem(K, NXL, NY, NZ), vmem(GROWS, NZ)),
        in_specs=[ANY, ANY] + [VM] * (3 + len(halos)),
        out_specs=(VM, VM),
        scratch_shapes=[
            window,
            pltpu.VMEM((2, 4, 7, TALL, NZ), F32),
            window,
            window,
            pltpu.VMEM((NP, 8, NZ), F32),
            pltpu.SemaphoreType.DMA((24,)),
        ],
        input_output_aliases={2: 0},
        compiler_params=PARAMS,
        name="adjoint_edges" if adjoint else "forward_edges",
    )(field, cf, block, edge, gram, *halos)


def finish_kernel(fin, ain, gf, g0, g1, fout, aout, lf, la, gs, coef, fo, ao, sem):
    row = lax.broadcasted_iota(jnp.int32, (K, NZ), 0)
    lane = lax.broadcasted_iota(jnp.int32, (K, NZ), 1)
    ga = g0[pl.ds(GROWS, GROWS)] + g1[pl.ds(GROWS, GROWS)]
    gs[0] = jnp.broadcast_to(jnp.sum(gf[pl.ds(0, GROWS)], axis=1, keepdims=True), (GROWS, NZ))
    gs[1] = jnp.broadcast_to(jnp.sum(ga, axis=1, keepdims=True), (GROWS, NZ))
    for s, ref in enumerate((lf, la)):
        a = {ij: jnp.broadcast_to(gs[s, p : p + 1, :], (8, NZ)) for p, ij in enumerate(PAIRS)}
        low, diag = {}, []
        for k in range(K):
            root = jnp.sqrt(a[k, k])
            low[k, k] = root
            diag.append(1.0 / root)
            for i in range(k + 1, K):
                low[i, k] = a[i, k] * diag[k]
            for i in range(k + 1, K):
                for j in range(k + 1, i + 1):
                    a[i, j] = a[i, j] - low[i, k] * low[j, k]
        matrix = jnp.zeros((K, NZ), F32)
        for i, j in PAIRS:
            matrix = jnp.where((row == i) & (lane == j), low[i, j], matrix)
        ref[...] = matrix[:, :K]
        inv = {}
        for j in range(K):
            inv[j, j] = diag[j]
            for i in range(j + 1, K):
                total = low[i, j] * inv[j, j]
                for m in range(j + 1, i):
                    total = total + low[i, m] * inv[m, j]
                inv[i, j] = -total * diag[i]
        for p, ij in enumerate(PAIRS):
            coef[s * NP + p] = inv[ij]
    c = Copies(sem)
    work = []
    for s, (src, dst, out) in enumerate(((fin, fo, fout), (ain, ao, aout))):
        for part in range(3):

            def body(p, carry, s=s, src=src, dst=dst):
                for t in range(NY // 8):
                    fields = [src[f, p, pl.ds(8 * t, 8)] for f in range(K)]
                    for i in range(K):
                        base = s * NP + i * (i + 1) // 2
                        total = coef[base] * fields[0]
                        for j in range(1, i + 1):
                            total = total + coef[base + j] * fields[j]
                        dst[i, p, pl.ds(8 * t, 8)] = total
                return carry

            lax.fori_loop(4 * part, 4 * part + 4, body, 0)
            planes = pl.ds(4 * part, 4)
            work.append(c.start(dst.at[:, planes], out.at[:, planes]))
    wait(work)


def finish(fin, ain, grams):
    block = pltpu.VMEM((K, NXL, NY, NZ), F32)
    shape = sds(K, NXL, NY, NZ)
    return pl.pallas_call(
        finish_kernel,
        out_shape=(shape, shape, sds(K, K), sds(K, K)),
        in_specs=[VM] * 5,
        out_specs=(ANY, ANY, VM, VM),
        scratch_shapes=[
            pltpu.VMEM((2, GROWS, NZ), F32),
            pltpu.VMEM((2 * NP, 8, NZ), F32),
            block,
            block,
            pltpu.SemaphoreType.DMA((6,)),
        ],
        compiler_params=PARAMS,
        name="finish",
    )(fin, ain, *grams)


def per_device(forward_sketch, adjoint_sketch, coefficients):
    peers, slices = lax.axis_size("space"), lax.axis_size("tm")
    fwd, adj, cf = (pltpu.with_memory_space_constraint(x[0], pltpu.HBM) for x in (forward_sketch, adjoint_sketch, coefficients))
    partner = [
        [(i, (i + 1 if (i % 2 == 1) == (k == 0) else i - 1) % peers) for i in range(peers)] for k in range(2)
    ]
    later = [(i, (i + 1) % slices) for i in range(slices)]
    earlier = [(j, i) for i, j in later]

    def hop(by, flip):
        return [
            (t * peers + s, ((t + by) % slices) * peers + (s ^ flip)) for t in range(slices) for s in range(peers)
        ]

    fhalo = [lax.ppermute(x, "space", partner[k]) for k, x in enumerate(pack(False, fwd, cf))]
    ahalo = [lax.ppermute(x, "space", partner[k]) for k, x in enumerate(pack(True, adj, cf))]
    fhalo, ahalo = [resident(x) for x in fhalo], [resident(x) for x in ahalo]
    fblock, ablock, fedge, aedge, fgram, agram = interior(fwd, adj, cf)
    fblock, fgram = edges(False, fwd, cf, fblock, fedge, fgram, fhalo)
    fgram = sum(lax.ppermute(fgram, ("tm", "space"), hop(1, flip)) for flip in (0, 8))
    ablock, agram = edges(True, adj, cf, ablock, aedge, agram, fhalo + ahalo)
    fblock = lax.ppermute(fblock, "tm", later)
    ablock = lax.ppermute(ablock, "tm", earlier)
    gram = jnp.concatenate([fgram, agram])
    for d in (1, 2, 7):
        gram = gram + lax.ppermute(gram, "space", [(i, i ^ d) for i in range(peers)])
    grams = [gram] + [lax.ppermute(gram, ("tm", "space"), hop(-1, flip)) for flip in (0, 8)]
    outs = finish(resident(fblock), resident(ablock), [resident(g) for g in grams])
    return tuple(o[None] for o in outs)


def solution(mesh):
    spec = P("tm", None, "space", None, None)
    return jax.shard_map(
        per_device,
        mesh=mesh,
        in_specs=(spec, spec, spec),
        out_specs=(spec, spec, P("tm", None, None), P("tm", None, None)),
        check_vma=False,
    )
```
